32 devices in a mesh: cells: 16 (over z, y, x), feat: 2 (over core).
Axes of the slice: x: 2, y: 2, z: 4, core: 2. Of those that a mesh axis runs over, the one named last changes fastest.
Arguments:
- features: float32 [32768, 4096], P('cells', 'feat'), may hold values from -6 to 6
- labels: int32 [32768], P('cells'), may hold values from 0 to 7
- weights: float32 [8, 4096], P(None, 'feat'), may hold values from -0.09375 to 0.09375
Outputs:
- new_weights: float32 [8, 4096], P(None, 'feat')
- new_logits: float32 [8, 32768], P(None, 'cells')
The draws below stay inside these ranges and needn't reach their ends.
All inputs are finite; a program needn't handle non-finite values.
Results may differ from the reference program's by a relative error of at most 0.00018.
Values sent between devices are 32-bit elements; how exact they have to be, the bound alone decides.
A program may use at most 64 MiB of HBM per device.

```python
import jax
import jax.numpy as jnp
from jax import lax

K = 8
F = 4096
ITERS = 2
NTOT = 32768


def touch_ends(result, rng, low, largest):
    spot = [jax.random.randint(jax.random.fold_in(rng, axis), (), 0, length) for axis, length in enumerate(result.shape)]
    longest = result.shape.index(max(result.shape))
    beside = spot[:longest] + [(spot[longest] + 1) % result.shape[longest]] + spot[longest + 1:]
    return result.at[tuple(spot)].set(low).at[tuple(beside)].set(largest)


def spiked(drawn, own_key, source, target, shards_of, factor):
    owner, partner = [(jnp.arange(drawn.shape[dim]) // (drawn.shape[dim] // shards_of)).reshape([-1 if axis == dim else 1 for axis in range(drawn.ndim)]) for dim in (source, target)]
    chosen = jax.random.permutation(own_key, shards_of)[partner]
    strong = (owner == chosen) | (owner == (partner + shards_of // 2) % shards_of)
    return jnp.where(strong, factor * drawn, drawn)


def levels(own_key, dims, shards, least, top_value):
    loudness = 1.0
    for dim, blocks in shards:
        steps = jax.random.uniform(jax.random.fold_in(jax.random.fold_in(own_key, 6), dim), (blocks,), jnp.float32, least / len(shards), top_value / len(shards))
        loudness = loudness * jnp.repeat(jnp.exp(steps), dims[dim] // blocks).reshape((-1,) + (1,) * (len(dims) - 1 - dim))
    return loudness


def noise(key, dims, deviation, most, split=(), kind=jnp.bfloat16):
    factor_of = levels(key, dims, split, -0.22, 0.18) if split else 1.0
    result = jax.random.normal(key, dims, jnp.float32) * deviation * factor_of
    return jnp.minimum(jnp.maximum(result, -most), most).astype(kind)


def noise_with(stream_key, dims, width, most, split, heavy, kind=jnp.bfloat16):
    entries = width * jax.random.normal(stream_key, dims, jnp.float32)
    if split:
        entries = entries * levels(stream_key, dims, split, -0.22, 0.18)
    return jnp.clip(spiked(entries, jax.random.fold_in(stream_key, 3), *heavy), -most, most).astype(kind)


def setup_inputs(seed: int = 0) -> dict:
    key_list = jax.random.split(jax.random.key(seed), 4)
    features = noise_with(key_list[0], (NTOT, F), 1.0, 6.0, ((0, 16), (1, 2)), (0, 1, 16, 2.0), jnp.float32)
    labels = touch_ends(jax.random.randint(key_list[1], (NTOT,), 0, K), jax.random.fold_in(key_list[1], 1), 0, K - 1).astype(jnp.int32)
    weights = noise(key_list[2], (K, F), F ** -0.5, 0.09375, ((1, 2),), jnp.float32)
    return {"features": features, "labels": labels, "weights": weights}


HIGH = lax.Precision.HIGHEST
RIDGE = 0.01


def scores(coeffs, features):
    return lax.dot_general(coeffs, features, (((1,), (1,)), ((), ())), precision=HIGH, preferred_element_type=jnp.float32)


def reference(features, labels, weights):
    count = features.shape[0] * 1.0
    logits = scores(weights, features)
    expo = jnp.exp(logits)
    probs = expo / jnp.sum(expo, axis=0, keepdims=True)
    onehot = (labels[None, :] == jnp.arange(K, dtype=jnp.int32)[:, None]).astype(jnp.float32)
    grad = jnp.dot(probs - onehot, features, precision=HIGH) / count + RIDGE * weights
    resid = -grad
    direction = resid
    rr_now = jnp.sum(resid * resid)
    step = jnp.zeros_like(weights)
    moved = jnp.zeros_like(logits)
    for it in range(ITERS):
        image = scores(direction, features)
        curv = probs * image - probs * jnp.sum(probs * image, axis=0, keepdims=True)
        product = jnp.dot(curv, features, precision=HIGH) / count + RIDGE * direction
        alpha = rr_now / jnp.sum(direction * product)
        step = step + alpha * direction
        moved = moved + alpha * image
        resid = resid - alpha * product
        if it + 1 < ITERS:
            rr_next = jnp.sum(resid * resid)
            direction = resid + (rr_next / rr_now) * direction
            rr_now = rr_next
    return weights + step, logits + moved
```

```python
import functools

import jax
import jax.numpy as jnp
from jax import lax
from jax.experimental import pallas as pl
from jax.experimental.pallas import tpu as pltpu
from jax.sharding import PartitionSpec as P

RIDGE = 0.01
MESH = pl.DeviceIdType.MESH
F32 = jnp.float32
BF16 = jnp.bfloat16


def split2(v):
    hi = v.astype(BF16)
    lo = (v - hi.astype(F32)).astype(BF16)
    return hi, lo


def stack2(v):
    hi = v.astype(BF16).astype(F32)
    return jnp.concatenate([hi, v - hi], axis=0).astype(BF16)


def total(v):
    return jnp.sum(jnp.sum(v, axis=1, keepdims=True), axis=0, keepdims=True)


def kernel(
    ncells, nfeat, count,
    x_hbm, lab_ref, w_ref, neww_ref, newl_ref,
    xs, xhi, xlo, part, logits, probs, image, t16, c16, gpart, rs, gbuf, qpart, rs2, qbuf,
    sc_f, sc_c,
    load_sem, fs_send, fs_recv, fsc_send, fsc_recv, rs_send, rs_recv, ag_send, ag_recv, cs_send, cs_recv,
):
    K, F = w_ref.shape
    NC, CH = xs.shape[0], xs.shape[1]
    W = rs.shape[2]
    owners = F // W
    TN = min(2 * W, F)
    per = TN // W
    tiles = F // TN
    KB = min(512, F)
    me = lax.axis_index("cells")
    mf = lax.axis_index("feat")

    loads = [pltpu.make_async_copy(x_hbm.at[pl.ds(i * CH, CH), :], xs.at[i], load_sem.at[i]) for i in range(NC)]
    for cp in loads:
        cp.start()
    barrier = pltpu.get_barrier_semaphore()
    for d in range(1, ncells):
        pl.semaphore_signal(barrier, inc=1, device_id={"cells": lax.rem(me + d, ncells)}, device_id_type=MESH)
    for d in range(1, nfeat):
        pl.semaphore_signal(barrier, inc=1, device_id={"feat": lax.rem(mf + d, nfeat)}, device_id_type=MESH)

    def feat_copy(ph, i, d, to):
        other = lax.rem(mf + d, nfeat)
        slot = mf if to else other
        return pltpu.make_async_remote_copy(
            src_ref=part.at[ph, i, mf], dst_ref=part.at[ph, i, slot],
            send_sem=fs_send.at[ph, i, other], recv_sem=fs_recv.at[ph, i, slot],
            device_id={"feat": other}, device_id_type=MESH)

    def feat_start(ph, i):
        for d in range(1, nfeat):
            feat_copy(ph, i, d, True).start()

    def feat_sum(ph, i):
        for d in range(1, nfeat):
            feat_copy(ph, i, d, False).wait_recv()
        out = part[ph, i, 0]
        for s in range(1, nfeat):
            out = out + part[ph, i, s]
        return out

    def fsc_copy(ph, d, to):
        other = lax.rem(mf + d, nfeat)
        slot = mf if to else other
        return pltpu.make_async_remote_copy(
            src_ref=sc_f.at[ph, mf], dst_ref=sc_f.at[ph, slot],
            send_sem=fsc_send.at[ph, other], recv_sem=fsc_recv.at[ph, slot],
            device_id={"feat": other}, device_id_type=MESH)

    def fsc_start(ph, a, b):
        rows = lax.broadcasted_iota(jnp.int32, (8, 128), 0)
        sc_f[ph, mf] = jnp.where(rows == 0, jnp.broadcast_to(a, (8, 128)), jnp.broadcast_to(b, (8, 128)))
        for d in range(1, nfeat):
            fsc_copy(ph, d, True).start()

    def fsc_sum(ph):
        for d in range(1, nfeat):
            fsc_copy(ph, d, False).wait_recv()
        out = sc_f[ph, 0]
        for s in range(1, nfeat):
            out = out + sc_f[ph, s]
        return out[0:1, 0:1], out[1:2, 0:1]

    def cs_copy(ph, d, to):
        other = lax.rem(me + d, ncells)
        slot = me if to else other
        return pltpu.make_async_remote_copy(
            src_ref=sc_c.at[ph, me], dst_ref=sc_c.at[ph, slot],
            send_sem=cs_send.at[ph, other], recv_sem=cs_recv.at[ph, slot],
            device_id={"cells": other}, device_id_type=MESH)

    def cs_start(ph, a):
        sc_c[ph, me] = jnp.broadcast_to(a, (8, 128))
        for d in range(1, ncells):
            cs_copy(ph, d, True).start()

    def cs_sum(ph):
        for d in range(1, ncells):
            cs_copy(ph, d, False).wait_recv()
        out = sc_c[ph, 0]
        for s in range(1, ncells):
            out = out + sc_c[ph, s]
        return out[0:1, 0:1]

    def rs_copy(ph, part_ref, buf, owner):
        return pltpu.make_async_remote_copy(
            src_ref=part_ref.at[:, pl.ds(pl.multiple_of(owner * W, W), W)], dst_ref=buf.at[me],
            send_sem=rs_send.at[ph, owner], recv_sem=rs_recv.at[ph, me],
            device_id={"cells": owner}, device_id_type=MESH)

    def rs_wait(ph, part_ref, buf, d):
        src = lax.rem(me + d, ncells)
        pltpu.make_async_remote_copy(
            src_ref=part_ref.at[:, pl.ds(0, W)], dst_ref=buf.at[src],
            send_sem=rs_send.at[ph, 0], recv_sem=rs_recv.at[ph, src],
            device_id={"cells": src}, device_id_type=MESH).wait_recv()

    def ag_copy(ph, buf, d):
        sl = buf.at[:, pl.ds(pl.multiple_of(me * W, W), W)]
        return pltpu.make_async_remote_copy(
            src_ref=sl, dst_ref=sl, send_sem=ag_send.at[ph, d], recv_sem=ag_recv.at[ph, me],
            device_id={"cells": lax.rem(me + d, ncells)}, device_id_type=MESH)

    def ag_wait(ph, buf, src):
        sl = buf.at[:, pl.ds(pl.multiple_of(src * W, W), W)]
        pltpu.make_async_remote_copy(
            src_ref=sl, dst_ref=sl, send_sem=ag_send.at[ph, 0], recv_sem=ag_recv.at[ph, src],
            device_id={"cells": src}, device_id_type=MESH).wait_recv()

    def collect(ph, part_ref, rsbuf, buf, add_ref, sign):
        first = lax.rem(me, owners) // per

        @pl.loop(0, tiles)
        def _(j):
            tile = lax.rem(first + j, tiles)
            cols = pl.ds(pl.multiple_of(tile * TN, TN), TN)
            t = t16[...]
            acc = jnp.dot(t, xhi[:, cols], preferred_element_type=F32)
            acc += jnp.dot(t, xlo[:, cols], preferred_element_type=F32)
            part_ref[:, cols] = acc[:K] + acc[K:]
            for u in range(per):
                owner = tile * per + u

                @pl.when(owner != me)
                def _():
                    rs_copy(ph, part_ref, rsbuf, owner).start()

        mine = pl.ds(pl.multiple_of(lax.rem(me, owners) * W, W), W)

        @pl.when(me < owners)
        def _():
            rsbuf[me] = part_ref[:, mine]
            for d in range(1, ncells):
                rs_wait(ph, part_ref, rsbuf, d)
            acc = rsbuf[0]
            for s in range(1, ncells):
                acc = acc + rsbuf[s]
            buf[:, mine] = sign * (acc / count) + RIDGE * add_ref[:, mine]
            for d in range(1, ncells):
                ag_copy(ph, buf, d).start()

        for s in range(owners):
            @pl.when(me != s)
            def _():
                ag_wait(ph, buf, s)

    def images(ph, i):
        rows = pl.ds(pl.multiple_of(i * CH, CH), CH)
        dims = (((1,), (1,)), ((), ()))
        c = c16[...]
        acc = lax.dot_general(c, xhi[rows, :], dims, preferred_element_type=F32)
        acc += lax.dot_general(c, xlo[rows, :], dims, preferred_element_type=F32)
        part[ph, i, mf] = acc[:K] + acc[K:]

    c16[...] = stack2(w_ref[...])
    for i in range(NC):
        loads[i].wait()

        @pl.loop(0, F // KB)
        def _(b):
            cols = pl.ds(pl.multiple_of(b * KB, KB), KB)
            hi, lo = split2(xs[i, :, cols])
            xhi[pl.ds(i * CH, CH), cols] = hi
            xlo[pl.ds(i * CH, CH), cols] = lo

        images(0, i)
        if i == 0:
            pl.semaphore_wait(barrier, ncells - 1 + nfeat - 1)
        feat_start(0, i)

    for i in range(NC):
        lg = feat_sum(0, i)
        e = jnp.exp(lg)
        p = e / jnp.sum(e, axis=0, keepdims=True)
        lab = lab_ref[:, pl.ds(i * CH, CH)]
        hot = (jnp.broadcast_to(lab, (K, CH)) == lax.broadcasted_iota(jnp.int32, (K, CH), 0)).astype(F32)
        logits[i] = lg
        probs[i] = p
        t16[:, pl.ds(i * CH, CH)] = stack2(p - hot)
    collect(0, gpart, rs, gbuf, w_ref, 1.0)

    g = gbuf[...]
    gbuf_neg = -g
    c16[...] = stack2(gbuf_neg)
    rr_part = total(g * g)
    fsc_start(0, rr_part, jnp.zeros_like(rr_part))

    @pl.loop(0, NC)
    def _(i):
        images(1, i)
        feat_start(1, i)

    s1 = jnp.zeros((1, 1), F32)
    for i in range(NC):
        im = feat_sum(1, i)
        p = probs[i]
        pim = p * im
        curv = pim - p * jnp.sum(pim, axis=0, keepdims=True)
        image[i] = im
        s1 = s1 + total(im * curv)
        t16[:, pl.ds(i * CH, CH)] = stack2(curv)
    cs_start(0, s1)
    rr, _ = fsc_sum(0)
    neww_ref[...] = -gbuf[...]
    collect(1, qpart, rs2, qbuf, neww_ref, 1.0)
    alpha = rr / (cs_sum(0) / count + RIDGE * rr)

    d1 = -gbuf[...]
    r1 = d1 - alpha * qbuf[...]
    c16[...] = stack2(r1)
    fsc_start(1, total(r1 * r1), total(r1 * d1))

    @pl.loop(0, NC)
    def _(i):
        images(2, i)
        feat_start(2, i)

    rr1, rd = fsc_sum(1)
    beta = rr1 / rr
    s2 = jnp.zeros((1, 1), F32)
    for i in range(NC):
        im1 = image[i]
        im = feat_sum(2, i) + beta * im1
        p = probs[i]
        pim = p * im
        curv = pim - p * jnp.sum(pim, axis=0, keepdims=True)
        s2 = s2 + total(im * curv)
        logits[i] = logits[i] + alpha * im1
        image[i] = im
    cs_start(1, s2)
    dd2 = rr1 + 2.0 * beta * rd + beta * beta * rr
    d1 = -gbuf[...]
    d2 = d1 - alpha * qbuf[...] + beta * d1
    first = w_ref[...] + alpha * d1
    alpha2 = rr1 / (cs_sum(1) / count + RIDGE * dd2)
    neww_ref[...] = first + alpha2 * d2
    for i in range(NC):
        newl_ref[:, pl.ds(i * CH, CH)] = logits[i] + alpha2 * image[i]

    for ph in range(3):
        for i in range(NC):
            for d in range(1, nfeat):
                feat_copy(ph, i, d, True).wait_send()
    for ph in range(2):
        for d in range(1, nfeat):
            fsc_copy(ph, d, True).wait_send()
        for d in range(1, ncells):
            cs_copy(ph, d, True).wait_send()
        pr, rb, bb = ((gpart, rs, gbuf), (qpart, rs2, qbuf))[ph]
        for s in range(owners):
            @pl.when(me != s)
            def _():
                rs_copy(ph, pr, rb, s).wait_send()

        @pl.when(me < owners)
        def _():
            for d in range(1, ncells):
                ag_copy(ph, bb, d).wait_send()


def on_device(ncells, nfeat, features, labels, weights):
    rows, F = features.shape
    K = weights.shape[0]
    NC = 8 if rows % 1024 == 0 else 1
    CH = rows // NC
    W = max(128, F // ncells)
    count = rows * ncells * 1.0
    vm = pltpu.VMEM
    dma = pltpu.SemaphoreType.DMA
    vmem = pl.BlockSpec(memory_space=pltpu.VMEM)
    return pl.pallas_call(
        functools.partial(kernel, ncells, nfeat, count),
        out_shape=(jax.ShapeDtypeStruct((K, F), F32), jax.ShapeDtypeStruct((K, rows), F32)),
        in_specs=[pl.BlockSpec(memory_space=pl.ANY), vmem, vmem],
        out_specs=(vmem, vmem),
        scratch_shapes=[
            vm((NC, CH, F), F32), vm((rows, F), BF16), vm((rows, F), BF16),
            vm((3, NC, nfeat, K, CH), F32), vm((NC, K, CH), F32), vm((NC, K, CH), F32), vm((NC, K, CH), F32),
            vm((2 * K, rows), BF16), vm((2 * K, F), BF16),
            vm((K, F), F32), vm((ncells, K, W), F32), vm((K, F), F32),
            vm((K, F), F32), vm((ncells, K, W), F32), vm((K, F), F32),
            vm((2, nfeat, 8, 128), F32), vm((2, ncells, 8, 128), F32),
            dma((NC,)), dma((3, NC, nfeat)), dma((3, NC, nfeat)), dma((2, nfeat)), dma((2, nfeat)),
            dma((2, ncells)), dma((2, ncells)), dma((2, ncells)), dma((2, ncells)), dma((2, ncells)), dma((2, ncells)),
        ],
        compiler_params=pltpu.CompilerParams(
            collective_id=0, has_side_effects=True, vmem_limit_bytes=56 * 1024 * 1024),
    )(features, labels[None, :], weights)


def solution(mesh):
    return jax.shard_map(
        functools.partial(on_device, mesh.shape["cells"], mesh.shape["feat"]),
        mesh=mesh,
        in_specs=(P("cells", "feat"), P("cells"), P(None, "feat")),
        out_specs=(P(None, "feat"), P(None, "cells")),
        check_vma=False,
    )
```

```python
import functools

import jax
import jax.numpy as jnp
from jax import lax
from jax.experimental import pallas as pl
from jax.experimental.pallas import tpu as pltpu
from jax.sharding import PartitionSpec as P

RIDGE = 0.01
MESH = pl.DeviceIdType.MESH
F32 = jnp.float32
BF16 = jnp.bfloat16


def split2(v):
    hi = v.astype(BF16)
    lo = (v - hi.astype(F32)).astype(BF16)
    return hi, lo


def stack2(v):
    hi = v.astype(BF16).astype(F32)
    return jnp.concatenate([hi, v - hi], axis=0).astype(BF16)


def total(v):
    return jnp.sum(jnp.sum(v, axis=1, keepdims=True), axis=0, keepdims=True)


def kernel(
    ncells, nfeat, count,
    x_hbm, lab_ref, w_ref, neww_ref, newl_ref,
    xs, xhi, xlo, thi, tlo, part, logits, probs, image, t16, c16, gpart, rs, gbuf, qpart, rs2, qbuf,
    sc_f, sc_c,
    load_sem, fs_send, fs_recv, fsc_send, fsc_recv, rs_send, rs_recv, ag_send, ag_recv, cs_send, cs_recv,
):
    K, F = w_ref.shape
    NC, CH = xs.shape[0], xs.shape[1]
    W = rs.shape[2]
    owners = F // W
    TN = min(4 * W, F)
    per = TN // W
    tiles = F // TN
    KB = min(256, F)
    me = lax.axis_index("cells")
    mf = lax.axis_index("feat")

    def ranked(j, own, n):
        above, below = n - 1 - own, own
        up = jnp.where(j < above, n - 1 - j, j - above)
        down = jnp.where(j < below, j, n - 1 - (j - below))
        return jnp.where(2 * own < n, up, down)

    loads = [pltpu.make_async_copy(x_hbm.at[pl.ds(i * CH, CH), :], xs.at[i], load_sem.at[i]) for i in range(NC)]
    for cp in loads:
        cp.start()
    barrier = pltpu.get_barrier_semaphore()
    for d in range(1, ncells):
        pl.semaphore_signal(barrier, inc=1, device_id={"cells": ranked(d - 1, me, ncells)}, device_id_type=MESH)
    for d in range(1, nfeat):
        pl.semaphore_signal(barrier, inc=1, device_id={"feat": lax.rem(mf + d, nfeat)}, device_id_type=MESH)

    mid = lax.rem(me, owners) // per

    def far_first(j):
        return ranked(j, mid, tiles)

    def feat_copy(ph, i, d, to):
        other = lax.rem(mf + d, nfeat)
        slot = mf if to else other
        return pltpu.make_async_remote_copy(
            src_ref=part.at[ph, i, mf], dst_ref=part.at[ph, i, slot],
            send_sem=fs_send.at[ph, i, other], recv_sem=fs_recv.at[ph, i, slot],
            device_id={"feat": other}, device_id_type=MESH)

    def feat_start(ph, i):
        for d in range(1, nfeat):
            feat_copy(ph, i, d, True).start()

    def feat_sum(ph, i):
        for d in range(1, nfeat):
            feat_copy(ph, i, d, False).wait_recv()
        out = part[ph, i, 0]
        for s in range(1, nfeat):
            out = out + part[ph, i, s]
        return out

    def fsc_copy(ph, d, to):
        other = lax.rem(mf + d, nfeat)
        slot = mf if to else other
        return pltpu.make_async_remote_copy(
            src_ref=sc_f.at[ph, mf], dst_ref=sc_f.at[ph, slot],
            send_sem=fsc_send.at[ph, other], recv_sem=fsc_recv.at[ph, slot],
            device_id={"feat": other}, device_id_type=MESH)

    def fsc_start(ph, a, b):
        rows = lax.broadcasted_iota(jnp.int32, (8, 128), 0)
        sc_f[ph, mf] = jnp.where(rows == 0, jnp.broadcast_to(a, (8, 128)), jnp.broadcast_to(b, (8, 128)))
        for d in range(1, nfeat):
            fsc_copy(ph, d, True).start()

    def fsc_sum(ph):
        for d in range(1, nfeat):
            fsc_copy(ph, d, False).wait_recv()
        out = sc_f[ph, 0]
        for s in range(1, nfeat):
            out = out + sc_f[ph, s]
        return out[0:1, 0:1], out[1:2, 0:1]

    def cs_copy(ph, d, to):
        other = ranked(d - 1, me, ncells)
        slot = me if to else other
        return pltpu.make_async_remote_copy(
            src_ref=sc_c.at[ph, me], dst_ref=sc_c.at[ph, slot],
            send_sem=cs_send.at[ph, other], recv_sem=cs_recv.at[ph, slot],
            device_id={"cells": other}, device_id_type=MESH)

    def cs_start(ph, a):
        sc_c[ph, me] = jnp.broadcast_to(a, (8, 128))
        for d in range(1, ncells):
            cs_copy(ph, d, True).start()

    def cs_sum(ph):
        for d in range(1, ncells):
            cs_copy(ph, d, False).wait_recv()
        out = sc_c[ph, 0]
        for s in range(1, ncells):
            out = out + sc_c[ph, s]
        return out[0:1, 0:1]

    def rs_copy(ph, part_ref, buf, owner):
        return pltpu.make_async_remote_copy(
            src_ref=part_ref.at[:, pl.ds(pl.multiple_of(owner * W, W), W)], dst_ref=buf.at[me],
            send_sem=rs_send.at[ph, owner], recv_sem=rs_recv.at[ph, me],
            device_id={"cells": owner}, device_id_type=MESH)

    def rs_wait(ph, part_ref, buf, d):
        src = lax.rem(me + d, ncells)
        pltpu.make_async_remote_copy(
            src_ref=part_ref.at[:, pl.ds(0, W)], dst_ref=buf.at[src],
            send_sem=rs_send.at[ph, 0], recv_sem=rs_recv.at[ph, src],
            device_id={"cells": src}, device_id_type=MESH).wait_recv()

    def ag_copy(ph, buf, d):
        sl = buf.at[:, pl.ds(pl.multiple_of(me * W, W), W)]
        return pltpu.make_async_remote_copy(
            src_ref=sl, dst_ref=sl, send_sem=ag_send.at[ph, d], recv_sem=ag_recv.at[ph, me],
            device_id={"cells": ranked(d - 1, me, ncells)}, device_id_type=MESH)

    def ag_wait(ph, buf, src):
        sl = buf.at[:, pl.ds(pl.multiple_of(src * W, W), W)]
        pltpu.make_async_remote_copy(
            src_ref=sl, dst_ref=sl, send_sem=ag_send.at[ph, 0], recv_sem=ag_recv.at[ph, src],
            device_id={"cells": src}, device_id_type=MESH).wait_recv()

    def collect(ph, part_ref, rsbuf, buf, add_ref, sign):
        @pl.loop(0, tiles)
        def _(j):
            tile = far_first(j)
            cols = pl.ds(pl.multiple_of(tile * TN, TN), TN)
            t = t16[...]
            acc = jnp.dot(t, xhi[:, cols], preferred_element_type=F32)
            acc += jnp.dot(t, xlo[:, cols], preferred_element_type=F32)
            part_ref[:, cols] = acc[:K] + acc[K:]
            for u in range(per):
                owner = tile * per + u

                @pl.when(owner != me)
                def _():
                    rs_copy(ph, part_ref, rsbuf, owner).start()

        mine = pl.ds(pl.multiple_of(lax.rem(me, owners) * W, W), W)

        @pl.when(me < owners)
        def _():
            rsbuf[me] = part_ref[:, mine]
            for d in range(1, ncells):
                rs_wait(ph, part_ref, rsbuf, d)
            acc = rsbuf[0]
            for s in range(1, ncells):
                acc = acc + rsbuf[s]
            buf[:, mine] = sign * (acc / count) + RIDGE * add_ref[:, mine]
            for d in range(1, ncells):
                ag_copy(ph, buf, d).start()

    def image_pass(ph, buf, coeffs):
        def one(j, last):
            tile = far_first(tiles - 1 - j)
            for u in range(per):
                owner = tile * per + u

                @pl.when(owner != me)
                def _():
                    ag_wait(ph - 1, buf, owner)
            cols = pl.ds(pl.multiple_of(tile * TN, TN), TN)
            c = stack2(coeffs(cols))
            for i in range(NC):
                acc = jnp.dot(c, thi[cols, pl.ds(i * CH, CH)], preferred_element_type=F32)
                acc += jnp.dot(c, tlo[cols, pl.ds(i * CH, CH)], preferred_element_type=F32)
                part[ph, i, mf] = part[ph, i, mf] + (acc[:K] + acc[K:])
                if last:
                    feat_start(ph, i)

        for i in range(NC):
            part[ph, i, mf] = jnp.zeros((K, CH), F32)
        if tiles > 1:
            @pl.loop(0, tiles - 1)
            def _(j):
                one(j, False)
        one(tiles - 1, True)

    c16[...] = stack2(w_ref[...])
    steps = F // KB
    unroll = 8 if steps % 8 == 0 else 1

    @pl.loop(0, NC)
    def _(i):
        pltpu.make_async_copy(x_hbm.at[pl.ds(0, CH), :], xs.at[i], load_sem.at[i]).wait()
        rows = pl.ds(pl.multiple_of(i * CH, CH), CH)
        part[0, i, mf] = jnp.zeros((K, CH), F32)

        @pl.loop(0, steps // unroll)
        def _(b):
            acc = jnp.zeros((2 * K, CH), F32)
            for v in range(unroll):
                cols = pl.ds(pl.multiple_of((b * unroll + v) * KB, KB), KB)
                hi, lo = split2(xs[i, :, cols])
                xhi[rows, cols] = hi
                xlo[rows, cols] = lo
                hit, lot = hi.T, lo.T
                thi[cols, rows] = hit
                tlo[cols, rows] = lot
                c = c16[:, cols]
                acc += jnp.dot(c, hit, preferred_element_type=F32)
                acc += jnp.dot(c, lot, preferred_element_type=F32)
            part[0, i, mf] = part[0, i, mf] + (acc[:K] + acc[K:])

        @pl.when(i == NC - 2)
        def _():
            pl.semaphore_wait(barrier, ncells - 1 + nfeat - 1)
            for k in range(NC - 2):
                feat_start(0, k)

        @pl.when(i >= NC - 2)
        def _():
            feat_start(0, i)

    for i in range(NC):
        lg = feat_sum(0, i)
        e = jnp.exp(lg)
        p = e / jnp.sum(e, axis=0, keepdims=True)
        lab = lab_ref[:, pl.ds(i * CH, CH)]
        hot = (jnp.broadcast_to(lab, (K, CH)) == lax.broadcasted_iota(jnp.int32, (K, CH), 0)).astype(F32)
        logits[i] = lg
        probs[i] = p
        t16[:, pl.ds(i * CH, CH)] = stack2(p - hot)
    collect(0, gpart, rs, gbuf, w_ref, 1.0)

    image_pass(1, gbuf, lambda cols: -gbuf[:, cols])
    g = gbuf[...]
    rr_part = total(g * g)
    fsc_start(0, rr_part, jnp.zeros_like(rr_part))
    neww_ref[...] = -g

    s1 = jnp.zeros((1, 1), F32)
    for i in range(NC):
        im = feat_sum(1, i)
        p = probs[i]
        pim = p * im
        curv = pim - p * jnp.sum(pim, axis=0, keepdims=True)
        image[i] = im
        s1 = s1 + total(im * curv)
        t16[:, pl.ds(i * CH, CH)] = stack2(curv)
    cs_start(0, s1)
    rr, _ = fsc_sum(0)
    collect(1, qpart, rs2, qbuf, neww_ref, 1.0)
    alpha = rr / (cs_sum(0) / count + RIDGE * rr)

    image_pass(2, qbuf, lambda cols: -gbuf[:, cols] - alpha * qbuf[:, cols])
    d1 = -gbuf[...]
    r1 = d1 - alpha * qbuf[...]
    fsc_start(1, total(r1 * r1), total(r1 * d1))

    rr1, rd = fsc_sum(1)
    beta = rr1 / rr
    s2 = jnp.zeros((1, 1), F32)
    for i in range(NC):
        im1 = image[i]
        im = feat_sum(2, i) + beta * im1
        p = probs[i]
        pim = p * im
        curv = pim - p * jnp.sum(pim, axis=0, keepdims=True)
        s2 = s2 + total(im * curv)
        logits[i] = logits[i] + alpha * im1
        image[i] = im
    cs_start(1, s2)
    dd2 = rr1 + 2.0 * beta * rd + beta * beta * rr
    d1 = -gbuf[...]
    d2 = d1 - alpha * qbuf[...] + beta * d1
    first = w_ref[...] + alpha * d1
    alpha2 = rr1 / (cs_sum(1) / count + RIDGE * dd2)
    neww_ref[...] = first + alpha2 * d2
    for i in range(NC):
        newl_ref[:, pl.ds(i * CH, CH)] = logits[i] + alpha2 * image[i]

    for ph in range(3):
        for i in range(NC):
            for d in range(1, nfeat):
                feat_copy(ph, i, d, True).wait_send()
    for ph in range(2):
        for d in range(1, nfeat):
            fsc_copy(ph, d, True).wait_send()
        for d in range(1, ncells):
            cs_copy(ph, d, True).wait_send()
        pr, rb, bb = ((gpart, rs, gbuf), (qpart, rs2, qbuf))[ph]
        for s in range(owners):
            @pl.when(me != s)
            def _():
                rs_copy(ph, pr, rb, s).wait_send()

        @pl.when(me < owners)
        def _():
            for d in range(1, ncells):
                ag_copy(ph, bb, d).wait_send()


def on_device(ncells, nfeat, features, labels, weights):
    rows, F = features.shape
    K = weights.shape[0]
    NC = 4 if rows % 512 == 0 else 2
    CH = rows // NC
    W = max(128, F // ncells)
    count = rows * ncells * 1.0
    vm = pltpu.VMEM
    dma = pltpu.SemaphoreType.DMA
    vmem = pl.BlockSpec(memory_space=pltpu.VMEM)
    return pl.pallas_call(
        functools.partial(kernel, ncells, nfeat, count),
        out_shape=(jax.ShapeDtypeStruct((K, F), F32), jax.ShapeDtypeStruct((K, rows), F32)),
        in_specs=[pl.BlockSpec(memory_space=pl.ANY), vmem, vmem],
        out_specs=(vmem, vmem),
        scratch_shapes=[
            vm((NC, CH, F), F32), vm((rows, F), BF16), vm((rows, F), BF16), vm((F, rows), BF16), vm((F, rows), BF16),
            vm((3, NC, nfeat, K, CH), F32), vm((NC, K, CH), F32), vm((NC, K, CH), F32), vm((NC, K, CH), F32),
            vm((2 * K, rows), BF16), vm((2 * K, F), BF16),
            vm((K, F), F32), vm((ncells, K, W), F32), vm((K, F), F32),
            vm((K, F), F32), vm((ncells, K, W), F32), vm((K, F), F32),
            vm((2, nfeat, 8, 128), F32), vm((2, ncells, 8, 128), F32),
            dma((NC,)), dma((3, NC, nfeat)), dma((3, NC, nfeat)), dma((2, nfeat)), dma((2, nfeat)),
            dma((2, ncells)), dma((2, ncells)), dma((2, ncells)), dma((2, ncells)), dma((2, ncells)), dma((2, ncells)),
        ],
        compiler_params=pltpu.CompilerParams(
            collective_id=0, has_side_effects=True, vmem_limit_bytes=56 * 1024 * 1024),
    )(features, labels[None, :], weights)


def solution(mesh):
    return jax.shard_map(
        functools.partial(on_device, mesh.shape["cells"], mesh.shape["feat"]),
        mesh=mesh,
        in_specs=(P("cells", "feat"), P("cells"), P(None, "feat")),
        out_specs=(P(None, "feat"), P(None, "cells")),
        check_vma=False,
    )
```
